256 devices in a mesh: section: 8 (over y, x_hi), ctx: 32 (over x_lo, z, core).
Axes of the slice: x: 4 (x_hi: 2, x_lo: 2; x = x_hi * 2 + x_lo), y: 4, z: 8, core: 2. Of those that a mesh axis runs over, the one named last changes fastest.
Arguments:
- queries: bfloat16 [8, 12288, 40, 128], P('section', 'ctx'), may hold values from -60 to 60
- keys_values: bfloat16 [12288, 2, 40, 128], P('ctx', None, 'section'), may hold values from -6 to 6
- positions: int32 [12288], P('ctx'), may hold values from 0 to 1533, as said below
- documents: int32 [12288], P('ctx'), may hold values from 0 to 12287, as said below
Outputs:
- attended: bfloat16 [8, 12288, 40, 128], P('section', 'ctx')
The draws below stay inside these ranges and needn't reach their ends.
Inputs may be any that keep to these rules, and one draw needn't show every extreme that they name: `documents`: Non-decreasing along the sequence; each document is a run of 1 to 384 tokens sharing one id, one document has exactly 384 tokens, and the last document's id is 12287. `positions`: within a document the ids rise by 1 to 3 from each token to the next; a document's first id is 0 to 384.
All inputs are finite; a program needn't handle non-finite values.
Results may differ from the reference program's by a relative error of at most 0.01.
Values may be sent and summed in bfloat16 or wider, within the bound.
A program may use at most 128 MiB of HBM per device.

```python
import jax
import jax.numpy as jnp
from jax import lax

HEADS = 40
HEAD_DIM = 128
TOK_DEV = 384
SECTIONS = 8
TOKENS = 12288


def doc_layout(key):
    length_key, offset_key, step_key = jax.random.split(jax.random.fold_in(key, 7), 3)
    lengths = jax.random.randint(length_key, (TOKENS,), 1, TOK_DEV + 1)
    doc_index = jnp.arange(TOKENS)
    lengths = jnp.where(doc_index == 0, TOK_DEV // 2, lengths)
    lengths = jnp.where(doc_index == 1, TOK_DEV, lengths).astype(jnp.int32)
    endings = jnp.cumsum(lengths)
    starting = endings - lengths
    token_index = jnp.arange(TOKENS, dtype=jnp.int32)
    doc_ids = (jnp.searchsorted(starting, token_index, side='right') - 1).astype(jnp.int32)
    strides = jax.random.randint(step_key, (TOKENS,), 1, 4).astype(jnp.int32)
    strides = jnp.where(doc_ids == 1, 3, strides).astype(jnp.int32)
    running = jnp.cumsum(strides).astype(jnp.int32)
    offsets = jax.random.randint(offset_key, (TOKENS,), 0, TOK_DEV + 1).astype(jnp.int32)
    offsets = jnp.where(doc_index == 0, 0, offsets)
    offsets = jnp.where(doc_index == 1, TOK_DEV, offsets).astype(jnp.int32)
    first_token = starting[doc_ids]
    position_ids = running - running[first_token] + offsets[doc_ids]
    last_doc = doc_ids[TOKENS - 1]
    doc_ids = jnp.where(doc_ids == last_doc, TOKENS - 1, doc_ids).astype(jnp.int32)
    return (doc_ids, position_ids.astype(jnp.int32))


def draw_documents(key, part):
    return doc_layout(key)[0]


def draw_positions(key, part):
    return doc_layout(key)[1]


def kv_base(key):
    kv_key = jax.random.fold_in(key, 11)
    array_shape = (TOKENS, 2, HEADS, HEAD_DIM)
    drawn = jnp.clip(jax.random.normal(kv_key, array_shape, jnp.float32), -6.0, 6.0)
    return drawn


def draw_keys_values(key, part):
    return kv_base(key).astype(jnp.bfloat16)


def draw_queries(key, part):
    array_shape = (SECTIONS, TOKENS, HEADS, HEAD_DIM)
    query_key = jax.random.fold_in(key, 13)
    drawn = jnp.clip(jax.random.normal(query_key, array_shape, jnp.float32), -6.0, 6.0)
    return drawn.astype(jnp.bfloat16)


def setup_inputs(seed: int = 0) -> dict:
    arg_keys = jax.random.split(jax.random.key(seed), 5)
    return {
        "queries": draw_queries(jax.random.fold_in(arg_keys[4], 71), 0),
        "keys_values": draw_keys_values(jax.random.fold_in(arg_keys[4], 71), 0),
        "positions": draw_positions(jax.random.fold_in(arg_keys[4], 71), 0),
        "documents": draw_documents(jax.random.fold_in(arg_keys[4], 71), 0),
    }


def rotate(values, token_positions):
    half_dim = values.shape[-1] // 2
    exponent = jnp.arange(half_dim, dtype=jnp.float32) * (2.0 / values.shape[-1])
    inverse = jnp.power(jnp.float32(10000.0), -exponent)
    angles = token_positions.astype(jnp.float32)[:, None] * inverse[None, :]
    cosine = jnp.cos(angles)[:, None, :]
    sine = jnp.sin(angles)[:, None, :]
    widened = values.astype(jnp.float32)
    lower = widened[..., :half_dim]
    upper = widened[..., half_dim:]
    joined = jnp.concatenate([lower * cosine - upper * sine, upper * cosine + lower * sine], axis=-1)
    return joined.astype(jnp.bfloat16)


def reference(queries, keys_values, positions, documents):
    rotated = rotate(queries, positions)
    cache_keys = rotate(keys_values[:, 0], positions)
    cache_values = keys_values[:, 1]
    padded_keys = jnp.concatenate([jnp.zeros((TOK_DEV, HEADS, HEAD_DIM), jnp.bfloat16), cache_keys], axis=0)
    padded_values = jnp.concatenate([jnp.zeros((TOK_DEV, HEADS, HEAD_DIM), jnp.bfloat16), cache_values], axis=0)
    padded_docs = jnp.concatenate([jnp.full((TOK_DEV,), -1, jnp.int32), documents.astype(jnp.int32)], axis=0)
    block_count = TOKENS // TOK_DEV
    scale = HEAD_DIM ** -0.5
    zero_index = jnp.zeros((), jnp.int32)
    causal = jnp.arange(2 * TOK_DEV)[None, :] <= jnp.arange(TOK_DEV)[:, None] + TOK_DEV

    def one_block(pair_index):
        section_index = (pair_index // block_count).astype(jnp.int32)
        row_start = ((pair_index % block_count) * TOK_DEV).astype(jnp.int32)
        query_block = lax.dynamic_slice(rotated, (section_index, row_start, zero_index, zero_index), (1, TOK_DEV, HEADS, HEAD_DIM))[0]
        key_block = lax.dynamic_slice_in_dim(padded_keys, row_start, 2 * TOK_DEV, 0)
        value_block = lax.dynamic_slice_in_dim(padded_values, row_start, 2 * TOK_DEV, 0)
        key_docs = lax.dynamic_slice_in_dim(padded_docs, row_start, 2 * TOK_DEV, 0)
        query_docs = lax.dynamic_slice_in_dim(documents.astype(jnp.int32), row_start, TOK_DEV, 0)
        allowed = jnp.logical_and(key_docs[None, :] == query_docs[:, None], causal)
        scores = jnp.einsum("qhd,khd->hqk", query_block.astype(jnp.float32), key_block.astype(jnp.float32)) * scale
        scores = jnp.where(allowed[None], scores, -1e30)
        largest = jnp.max(scores, axis=-1, keepdims=True)
        weights = jnp.exp(scores - largest)
        probs = (weights / jnp.sum(weights, axis=-1, keepdims=True)).astype(jnp.bfloat16)
        mixed = jnp.einsum("hqk,khd->qhd", probs.astype(jnp.float32), value_block.astype(jnp.float32))
        return mixed.astype(jnp.bfloat16)

    blocks_out = lax.map(one_block, jnp.arange(SECTIONS * block_count, dtype=jnp.int32))
    return blocks_out.reshape(SECTIONS, TOKENS, HEADS, HEAD_DIM)
```

```python
import functools

import jax
import jax.numpy as jnp
from jax import lax
from jax.experimental import pallas as pl
from jax.experimental.pallas import tpu as pltpu
from jax.sharding import PartitionSpec as P

MESH = pl.DeviceIdType.MESH
HOP = 1.8

OWN = ((0, 0, 3, 1, 1, 1), (0, 3, 2, 1, -1, -1), (1, 4, 1, 1, -1, -1), (1, 0, 2, 2, 1, 1), (1, 2, 2, 2, -1, -1))
PREV = ((0, 0, 3, 1, -1, -1), (0, 3, 2, 1, 1, 1), (1, 0, 3, 2, 1, 1), (1, 3, 2, 2, -1, -1))
CHUNKS = {"own": OWN, "prev": PREV}


def gather_tasks(core, stream, source_event):
    tasks = []

    def add(needs, link, units, event, what):
        tasks.append((core, needs, link, units, event, core, what))

    def along_y(chunk, units, turn, block, needs):
        for way in (turn, -turn):
            add(needs, ("y", way), units, (stream, "y1", way, block, chunk), ("ysend", stream, block, chunk, way))
        add(
            ((stream, "y1", turn, block, chunk),),
            ("y", turn),
            units,
            (stream, "y2", block, chunk),
            ("yfwd", stream, block, chunk, turn),
        )

    for chunk, (_, _, units, path, way, turn) in enumerate(CHUNKS[stream]):
        start = source_event(chunk)
        along_y(chunk, units, turn, 0, start)
        if path == 1:
            crossings = [(0, start, way)]
        else:
            crossings = [
                (0, start, way),
                (-1, ((stream, "y1", 1, 0, chunk),), -way),
                (2, ((stream, "y2", 0, chunk),), -way),
                (1, ((stream, "y1", -1, 0, chunk),), way),
            ]
        for row, needs, side in crossings:
            relay = (stream, "relay", row, chunk)
            add(needs, ("x", side), units, relay, ("xsend", stream, row, chunk, side))
            add((relay,), ("x", side), units, (stream, "x", row, chunk), ("xfwd", stream, row, chunk, side))
        if path == 1:
            along_y(chunk, units, turn, 1, ((stream, "x", 0, chunk),))
    return tasks


def all_tasks():
    tasks = gather_tasks(0, "own", lambda chunk: ()) + gather_tasks(1, "own", lambda chunk: ())
    for chunk, entry in enumerate(PREV):
        tasks.append((1, (), ("z", 1), entry[2], ("prev", "shift", chunk), 0, ("shift", "prev", chunk)))
    tasks += gather_tasks(0, "prev", lambda chunk: (("prev", "shift", chunk),))
    for chunk, (_, _, units, path, _, _) in enumerate(OWN):
        arrivals = [
            ((), 0, 0),
            ((("own", "y1", 1, 0, chunk),), -1, 0),
            ((("own", "y2", 0, chunk),), 2, 0),
            ((("own", "y1", -1, 0, chunk),), 1, 0),
        ]
        if path == 1:
            arrivals += [
                ((("own", "x", 0, chunk),), 0, 1),
                ((("own", "y1", 1, 1, chunk),), -1, 1),
                ((("own", "y2", 1, chunk),), 2, 1),
                ((("own", "y1", -1, 1, chunk),), 1, 1),
            ]
        else:
            arrivals += [((("own", "x", row, chunk),), row, 1) for row in (0, -1, 2, 1)]
        for needs, row, other in arrivals:
            event = ("pass", row, other, chunk)
            tasks.append((0, needs, ("core", 1), units, event, 1, ("pass", row, other, chunk)))
    return tasks


def issue_order(tasks):
    users = {}
    for task in tasks:
        for need in task[1]:
            users.setdefault((need, task[0]), []).append(task)

    @functools.lru_cache(None)
    def remaining(task):
        after = [remaining(user) for user in users.get((task[4], task[5]), []) if user[2][0] != "core"]
        return task[3] + 2.0 + max(after, default=0.0)

    step = 0.05
    pending = [[t for t in tasks if t[0] == core] for core in (0, 1)]
    order = ([], [])
    queues = {}
    arrived = {}
    now = 0.0
    while len(arrived) < len(tasks):
        for core in (0, 1):
            ready = [t for t in pending[core] if all(arrived.get((n, core), 1e9) <= now for n in t[1])]
            for task in sorted(ready, key=lambda t: -remaining(t)):
                queue = queues.setdefault((core, task[2]), [])
                if len(queue) < 3:
                    queue.append([task, 1.06 * task[3]])
                    pending[core].remove(task)
                    order[core].append(task)
        for link in {key[1] for key in queues}:
            active = [core for core in (0, 1) if queues.get((core, link))]
            for core in active:
                head = queues[(core, link)][0]
                head[1] -= step / len(active) * (5 if link[0] == "core" else 1)
                if head[1] <= 1e-9:
                    queues[(core, link)].pop(0)
                    arrived[(head[0][4], head[0][5])] = now + step + HOP
        now += step
    return order


def exchange(share_ref, docs_ref, whole_ref, prev_ref, prev_docs_ref, relay_ref, send_sem, recv_sem, local_sem):
    section = lax.axis_index("section")
    shard = lax.axis_index("ctx")
    shards = lax.axis_size("ctx")
    share_heads = share_ref.shape[1]
    y, x_hi = section // 2, section % 2
    core = shard % 2
    x_lo = shard // (shards // 2)
    inner = shard % (shards // 2)

    def along_x(way):
        flips = x_lo == (1 if way == 1 else 0)
        hi = jnp.where(flips, 1 - x_hi, x_hi)
        return hi, {"section": y * 2 + hi, "ctx": (1 - x_lo) * (shards // 2) + inner}

    x_side = {way: along_x(way) for way in (1, -1)}
    y_side = {way: {"section": ((y + way + 4) % 4) * 2 + x_hi, "ctx": shard} for way in (1, -1)}
    later = {"section": section, "ctx": (shard + 1) % shards}
    earlier = {"section": section, "ctx": (shard + shards - 1) % shards}

    barrier = pltpu.get_barrier_semaphore()
    for device in (x_side[1][1], x_side[-1][1], y_side[1], y_side[-1], later, earlier):
        pl.semaphore_signal(barrier, inc=1, device_id=device, device_id_type=MESH)
    pl.semaphore_wait(barrier, 6)

    tasks = all_tasks()
    event_ids = {}
    for task in tasks:
        event_ids.setdefault(task[4], len(event_ids))
    relay_slots, used = {}, 0
    for stream in ("own", "prev"):
        for chunk, entry in enumerate(CHUNKS[stream]):
            for row in (0,) if entry[3] == 1 else (0, -1, 2, 1):
                relay_slots[(stream, row, chunk)] = used
                used += entry[2]

    def row_section(row, hi):
        return ((y + row + 4) % 4) * 2 + hi

    def held(stream, chunk, at):
        kind, head, heads = CHUNKS[stream][chunk][:3]
        ref = whole_ref if stream == "own" else prev_ref
        return ref.at[kind, pl.ds(at * share_heads + head, heads)]

    def own_or_held(stream, chunk, row, hi):
        kind, head, heads = CHUNKS[stream][chunk][:3]
        if row == 0 and hi is x_hi and stream == "own":
            return share_ref.at[kind, pl.ds(head, heads)]
        return held(stream, chunk, row_section(row, hi))

    def relay(stream, row, chunk):
        return relay_ref.at[pl.ds(relay_slots[(stream, row, chunk)], CHUNKS[stream][chunk][2])]

    def ends(what):
        kind = what[0]
        if kind == "ysend":
            _, stream, block, chunk, way = what
            hi = x_hi if block == 0 else 1 - x_hi
            return own_or_held(stream, chunk, 0, hi), held(stream, chunk, row_section(0, hi)), y_side[way]
        if kind == "yfwd":
            _, stream, block, chunk, way = what
            at = row_section(-way, x_hi if block == 0 else 1 - x_hi)
            return held(stream, chunk, at), held(stream, chunk, at), y_side[way]
        if kind == "xsend":
            _, stream, row, chunk, way = what
            return own_or_held(stream, chunk, row, x_hi), relay(stream, row, chunk), x_side[way][1]
        if kind == "xfwd":
            _, stream, row, chunk, way = what
            return relay(stream, row, chunk), held(stream, chunk, row_section(row, x_side[-way][0])), x_side[way][1]
        if kind == "shift":
            part, head, heads = PREV[what[2]][:3]
            return share_ref.at[part, pl.ds(head, heads)], held("prev", what[2], section), later
        _, row, other, chunk = what
        part, head, heads = OWN[chunk][:3]
        at = row_section(row, x_hi if other == 0 else 1 - x_hi)
        target = prev_ref.at[part, pl.ds(at * share_heads + head, heads)]
        return own_or_held("own", chunk, row, x_hi if other == 0 else 1 - x_hi), target, later

    def copy_of(task, number):
        source, target, device = ends(task[6])
        return pltpu.make_async_remote_copy(
            src_ref=source,
            dst_ref=target,
            send_sem=send_sem.at[number],
            recv_sem=recv_sem.at[event_ids[task[4]]],
            device_id=device,
            device_id_type=MESH,
        )

    docs_copy = pltpu.make_async_remote_copy(
        src_ref=docs_ref,
        dst_ref=prev_docs_ref,
        send_sem=local_sem.at[1],
        recv_sem=local_sem.at[2],
        device_id=later,
        device_id_type=MESH,
    )
    docs_copy.start()
    for kind in (0, 1):
        pltpu.make_async_copy(
            share_ref.at[kind], whole_ref.at[kind, pl.ds(section * share_heads, share_heads)], local_sem.at[3 + kind]
        ).start()

    units = {task[4]: task[3] for task in tasks}

    def wait_event(event):
        place = relay_ref.at[pl.ds(0, units[event])]
        pltpu.make_async_copy(place, place, recv_sem.at[event_ids[event]]).wait()

    def run(own_core, order):
        waited = set()
        sent = []
        for number, task in enumerate(order):
            for need in task[1]:
                if need not in waited:
                    waited.add(need)
                    wait_event(need)
            copy = copy_of(task, number)
            copy.start()
            sent.append(copy)
        for task in tasks:
            if task[5] == own_core and task[4] not in waited:
                waited.add(task[4])
                wait_event(task[4])
        for copy in sent:
            copy.wait_send()

    orders = issue_order(tasks)
    for number in (0, 1):
        pl.when(core == number)(functools.partial(run, number, orders[number]))
    docs_copy.wait()
    for kind in (0, 1):
        pltpu.make_async_copy(
            share_ref.at[kind], whole_ref.at[kind, pl.ds(section * share_heads, share_heads)], local_sem.at[3 + kind]
        ).wait()


def gather_cache(share, documents, sections):
    _, heads, rows, dim = share.shape
    tasks = all_tasks()
    relay_units = sum(e[2] * (1 if e[3] == 1 else 4) for e in OWN + PREV)
    sends = max(sum(t[0] == core for t in tasks) for core in (0, 1))
    events = len({t[4] for t in tasks})
    cache = jax.ShapeDtypeStruct((2, heads * sections, rows, dim), share.dtype)
    docs = documents.reshape(-1, 128)
    vmem = pl.BlockSpec(memory_space=pltpu.VMEM)
    hbm = pl.BlockSpec(memory_space=pl.ANY)
    return pl.pallas_call(
        exchange,
        out_shape=(cache, cache, jax.ShapeDtypeStruct(docs.shape, docs.dtype)),
        in_specs=[vmem, vmem],
        out_specs=(hbm, hbm, vmem),
        scratch_shapes=[
            pltpu.VMEM((relay_units, rows, dim), share.dtype),
            pltpu.SemaphoreType.DMA((sends,)),
            pltpu.SemaphoreType.DMA((events,)),
            pltpu.SemaphoreType.DMA((5,)),
        ],
        compiler_params=pltpu.CompilerParams(collective_id=0, has_side_effects=True),
        name="exchange",
    )(share, docs)


def attention(rows, heads, q_ref, cos_ref, sin_ref, ko_ref, kp_ref, vo_ref, vp_ref, qd_ref, kd_ref, o_ref, qf, of, bias):
    window = rows + 128
    blocks = rows // 128
    dim = q_ref.shape[-1]

    @pl.when(pl.program_id(0) == 0)
    def _():
        for block in range(blocks):
            queries = pl.ds(block * 128, 128)
            keys = pl.ds(block * 128, window)
            at_query = lax.broadcasted_iota(jnp.int32, (128, window), 0) + rows
            at_key = lax.broadcasted_iota(jnp.int32, (128, window), 1)
            allowed = jnp.logical_and(kd_ref[:, keys] == qd_ref[queries, :], at_key <= at_query)
            bias[block] = jnp.where(allowed, 0.0, -1e30)

    qf[...] = q_ref[0].astype(jnp.float32)
    factor = dim ** (-0.5) * 1.4426950408889634
    for head in range(heads):
        values = qf[:, head, :]
        turned = values * cos_ref[...] + pltpu.roll(values, dim // 2, 1) * sin_ref[...]
        rotated = turned.astype(jnp.bfloat16)
        for block in range(blocks):
            first = block * 128
            last = first + 128
            query = rotated[first:last]
            contract = (((1,), (1,)), ((), ()))
            scores = jnp.concatenate(
                [
                    lax.dot_general(query, kp_ref[0, head, first:rows], contract, preferred_element_type=jnp.float32),
                    lax.dot_general(query, ko_ref[0, head, 0:last], contract, preferred_element_type=jnp.float32),
                ],
                axis=1,
            )
            scores = scores * factor + bias[block]
            largest = jnp.max(scores, axis=1, keepdims=True)
            weights = jnp.exp2(scores - largest)
            total = jnp.sum(weights, axis=1, keepdims=True)
            probs = weights.astype(jnp.bfloat16)
            mixed = jnp.dot(probs[:, : rows - first], vp_ref[0, head, first:rows], preferred_element_type=jnp.float32)
            mixed += jnp.dot(probs[:, rows - first :], vo_ref[0, head, 0:last], preferred_element_type=jnp.float32)
            of[first:last, head, :] = mixed / total
    o_ref[0] = of[...].astype(jnp.bfloat16)


def attend(queries, whole, prev, cosine, sine, documents, key_docs):
    _, rows, head_count, dim = queries.shape
    group = 8
    window = rows + 128
    q_spec = pl.BlockSpec((1, rows, group, dim), lambda g: (0, 0, g, 0))
    table = pl.BlockSpec((rows, dim), lambda g: (0, 0))
    keys = pl.BlockSpec((1, group, rows, dim), lambda g: (0, g, 0, 0))
    values = pl.BlockSpec((1, group, rows, dim), lambda g: (1, g, 0, 0))
    return pl.pallas_call(
        functools.partial(attention, rows, group),
        grid=(head_count // group,),
        out_shape=jax.ShapeDtypeStruct(queries.shape, queries.dtype),
        in_specs=[
            q_spec,
            table,
            table,
            keys,
            keys,
            values,
            values,
            pl.BlockSpec((rows, 1), lambda g: (0, 0)),
            pl.BlockSpec((1, 2 * rows), lambda g: (0, 0)),
        ],
        out_specs=q_spec,
        scratch_shapes=[
            pltpu.VMEM((rows, group, dim), jnp.float32),
            pltpu.VMEM((rows, group, dim), jnp.float32),
            pltpu.VMEM((rows // 128, 128, window), jnp.float32),
        ],
        name="attend",
    )(queries, cosine, sine, whole, prev, whole, prev, documents[:, None], key_docs[None, :])


def tables(positions, dim):
    half_dim = dim // 2
    exponent = jnp.arange(half_dim, dtype=jnp.float32) * (2.0 / dim)
    inverse = jnp.power(jnp.float32(10000.0), -exponent)
    angles = positions.astype(jnp.float32)[:, None] * inverse[None, :]
    cosine = jnp.cos(angles)
    sine = jnp.sin(angles)
    return jnp.concatenate([cosine, cosine], axis=1), jnp.concatenate([-sine, sine], axis=1)


def body(queries, keys_values, positions, documents):
    dim = queries.shape[-1]
    sections = lax.axis_size("section")
    cosine, sine = tables(positions, dim)
    by_head = jnp.transpose(keys_values, (1, 2, 0, 3))
    keys = by_head[0].astype(jnp.float32)
    swapped = jnp.concatenate([keys[..., dim // 2 :], keys[..., : dim // 2]], axis=-1)
    share = jnp.stack([(keys * cosine + swapped * sine).astype(jnp.bfloat16), by_head[1]], axis=0)
    whole, prev, prev_docs = gather_cache(share, documents, sections)
    at_start = lax.axis_index("ctx") == 0
    key_docs = jnp.concatenate([jnp.where(at_start, -1, prev_docs.reshape(-1)), documents], axis=0)
    return attend(queries, whole, prev, cosine, sine, documents, key_docs)


def solution(mesh):
    placed = (P("section", "ctx", None, None), P("ctx", None, "section", None), P("ctx"), P("ctx"))
    return jax.shard_map(
        body, mesh=mesh, in_specs=placed, out_specs=P("section", "ctx", None, None), check_vma=False
    )
```

```python
import functools

import jax
import jax.numpy as jnp
from jax import lax
from jax.experimental import pallas as pl
from jax.experimental.pallas import tpu as pltpu
from jax.sharding import PartitionSpec as P

MESH = pl.DeviceIdType.MESH
VMEM_LIMIT = 48 * 2**20
HOP = 1.8
WIRE = 1.12
HEAD_TIME = 0.45

CLASSES = ((0, 3), (3, 2))
CHUNKS = ((0, 0, 3, 0), (1, 0, 3, 0), (0, 3, 2, 1), (1, 3, 2, 1))
PLACES = tuple((row, other) for other in (0, 1) for row in (0, 1, -1, 2))
ROWS = (0, -1, 2, 1)

PATHS = {
    "G": {
        "own": ((1, 1, 1, True), (2, 1, -1, True), (1, -1, -1, False), (1, 1, -1, True)),
        "prev": (None, None, (2, 1, 1, False), (2, 1, -1, False)),
    },
    "A": {
        "own": ((1, -1, 1, False), (1, -1, -1, True), (1, -1, 1, True), (1, -1, -1, True)),
        "prev": (None, None, None, None),
    },
    "B": {
        "own": ((2, 1, -1, True), (2, 1, -1, True), (2, -1, -1, False), (1, 1, 1, True)),
        "prev": ((1, -1, 1, False), (2, -1, -1, False), (1, 1, -1, False), (2, -1, -1, False)),
    },
}
ACROSS = {"G": "G", "A": "B", "B": "A"}
ROLES = ("G0", "G1", "A0", "A1", "B0", "B1", "E1", "F1")


def arrival(chip, stream, chunk, row, other):
    path = PATHS[chip][stream][chunk][0]
    if (row, other) == (0, 0):
        return None if stream == "own" else ("prev", "shift", chunk)
    if other == 1 and (path == 2 or row == 0):
        return (stream, "x", row, chunk)
    if row == 2:
        return (stream, "y2", other, chunk)
    return (stream, "y1", -row, other, chunk)


def gather_tasks(chip, core, stream):
    tasks = []
    node, relay_node = chip + str(core), ACROSS[chip] + str(core)
    for chunk, settings in enumerate(PATHS[chip][stream]):
        if settings is None:
            continue
        path, way, turn, opposite = settings
        if core == 1:
            way, turn = -way if opposite else way, -turn
        units, group = CHUNKS[chunk][2:]

        def add(sender, receiver, needs, axis, side, event, what):
            needs = tuple(n for n in needs if n)
            tasks.append((sender, needs, (sender[0], axis, side), units, event, receiver, what, group))

        def along_y(block, start):
            for side in (turn, -turn):
                event = (stream, "y1", side, block, chunk)
                add(node, node, (start,), "y", side, event, ("ysend", stream, block, chunk, side))
            event = (stream, "y2", block, chunk)
            needs = ((stream, "y1", turn, block, chunk),)
            add(node, node, needs, "y", turn, event, ("yfwd", stream, block, chunk, turn))

        along_y(0, arrival(chip, stream, chunk, 0, 0))
        for row in ROWS if path == 2 else (0,):
            side = way if row in (0, 1) else -way
            event = (stream, "relay", row, chunk)
            needs = (arrival(chip, stream, chunk, row, 0),)
            add(node, relay_node, needs, "x", side, event, ("xsend", stream, row, chunk, side))
            what = ("xfwd", stream, row, chunk, side)
            add(relay_node, node, (event,), "x", side, (stream, "x", row, chunk), what)
        if path == 1:
            along_y(1, (stream, "x", 0, chunk))
    return tasks


def pass_tasks(sender, receiver, link, chunks):
    tasks = []
    for chunk in chunks:
        for row, other in PLACES:
            event = arrival(sender[0], "own", chunk, row, other)
            what = ("pass", row, other, chunk)
            needs = (event,) if event else ()
            tasks.append((sender, needs, link, CHUNKS[chunk][2], what, receiver, what, CHUNKS[chunk][3]))
    return tasks


def shift_task(sender, receiver, link, chunk):
    what = ("prev", "shift", chunk)
    return (sender, (), link, CHUNKS[chunk][2], what, receiver, ("shift", "prev", chunk), CHUNKS[chunk][3])


def all_tasks():
    tasks = []
    for chip in "GAB":
        for core in (0, 1):
            tasks += gather_tasks(chip, core, "own")
        tasks += gather_tasks(chip, 0, "prev")
        tasks += pass_tasks(chip + "0", chip + "1", (chip, "core", 1), range(len(CHUNKS)))
        above = "G0" if chip == "G" else "above" + chip
        for chunk, settings in enumerate(PATHS["G"]["prev"]):
            if settings is None:
                tasks += pass_tasks(chip + "1", above, (chip, "z", 1), (chunk,))
            else:
                tasks.append(shift_task(chip + "1", above, (chip, "z", 1), chunk))
    for chunk in range(len(CHUNKS)):
        tasks.append(shift_task("E1", "B0", ("A", "x", 1), chunk))
    return tasks


def unit_needs(node, row, other, group):
    events = []
    for chunk, entry in enumerate(CHUNKS):
        if entry[3] != group:
            continue
        events.append(arrival(node[0], "own", chunk, row, other))
        if node[1] == "1" or (node[0] == "G" and PATHS["G"]["prev"][chunk] is None):
            events.append(("pass", row, other, chunk))
        elif node[0] != "A":
            events.append(arrival(node[0], "prev", chunk, row, other))
    return tuple(e for e in events if e)


def plan(tasks):
    users = {}
    for task in tasks:
        for need in task[1]:
            users.setdefault((need, task[0]), []).append(task)

    @functools.lru_cache(None)
    def remaining(task):
        after = [remaining(u) for u in users.get((task[4], task[5]), []) if u[6][0] != "pass"]
        return WIRE * task[3] + 2.0 + max(after, default=0.0)

    step = 0.05
    nodes = ("G0", "G1", "A0", "A1", "B0", "B1")
    pending = {n: sorted((t for t in tasks if t[0] == n), key=lambda t: 10 * t[7] - remaining(t)) for n in nodes}
    first = {n: [("turn", 0, 2, 3.0, 3.0), ("turn", 2, 5, 7.0, 4.5), ("mask", 0, 0, 7.0, 1.0)] for n in nodes}
    units = {n: [(g, place) for g in range(len(CLASSES)) for place in PLACES] for n in nodes}
    order = {n: [] for n in nodes}
    queues, arrived = {}, {}
    for task in tasks:
        if task[0] == "E1":
            queues.setdefault(task[2], {}).setdefault("E1", []).append([task, WIRE * task[3]])
    free = {n: 0.0 for n in nodes}
    now = 0.0
    while len(arrived) < len(tasks) or any(units.values()):
        for node in nodes:
            if free[node] > now:
                continue
            here = lambda events: all(arrived.get((e, node), 1e9) <= now for e in events)
            for task in [t for t in pending[node] if here(t[1])]:
                queue = queues.setdefault(task[2], {}).setdefault(node, [])
                if len(queue) < 3:
                    queue.append([task, WIRE * task[3]])
                    pending[node].remove(task)
                    order[node].append(("send", task))
            if first[node]:
                if first[node][0][3] <= now:
                    stage = first[node].pop(0)
                    free[node] = now + stage[4]
                    order[node].append(("stage", stage))
                continue
            group = units[node][0][0] if units[node] else 0
            able = [u for u in units[node] if u[0] == group and here(unit_needs(node, *u[1], u[0]))]
            if able:
                units[node].remove(able[0])
                free[node] = now + HEAD_TIME * CLASSES[group][1]
                order[node].append(("stage", ("unit", able[0])))
        for link in sorted(queues):
            active = [queue for queue in queues[link].values() if queue]
            for queue in active:
                entry = queue[0]
                entry[1] -= step / len(active) * (5 if link[1] == "core" else 1)
                if entry[1] <= 1e-9:
                    queue.pop(0)
                    arrived[(entry[0][4], entry[0][5])] = now + step + HOP
        now += step
    return order, now


def role_order(order, tasks, role):
    if role not in ("E1", "F1"):
        return order[role]
    kept = [e for e in order["G1"] if e[0] == "stage" or e[1][6][0] not in ("pass", "shift")]
    shifts = [("send", t) for t in tasks if t[0] == role]
    return shifts + kept


def head_scores(q_ref, whole_ref, prev_ref, bias_ref, head, block):
    rows, dim = q_ref.shape[1:]
    first, last = block * 128, block * 128 + 128
    contract = (((1,), (1,)), ((), ()))
    query = q_ref[head, first:last]
    scores = jnp.concatenate(
        [
            lax.dot_general(query, prev_ref[0, head, first:rows], contract, preferred_element_type=jnp.float32),
            lax.dot_general(query, whole_ref[0, head, 0:last], contract, preferred_element_type=jnp.float32),
        ],
        axis=1,
    )
    return scores * (dim ** (-0.5) * 1.4426950408889634) + bias_ref[block]


def head_values(scores, whole_ref, prev_ref, out_ref, head, block):
    heads, rows = whole_ref.shape[1:3]
    first, last = block * 128, block * 128 + 128
    largest = jnp.max(scores, axis=1, keepdims=True)
    weights = jnp.exp2(scores - largest)
    total = jnp.sum(weights, axis=1, keepdims=True)
    probs = weights.astype(jnp.bfloat16)
    mixed = jnp.dot(probs[:, : rows - first], prev_ref[1, head, first:rows], preferred_element_type=jnp.float32)
    mixed += jnp.dot(probs[:, rows - first :], whole_ref[1, head, 0:last], preferred_element_type=jnp.float32)
    out_ref[pl.ds(first * heads + head, 128, stride=heads), :] = mixed / total


def softmax_heads(q_ref, whole_ref, prev_ref, bias_ref, out_ref, heads):
    waiting = []
    for head in heads:
        for block in range(q_ref.shape[1] // 128):
            scores = head_scores(q_ref, whole_ref, prev_ref, bias_ref, head, block)
            waiting.append((scores, head, block))
            if len(waiting) > 3:
                scores, *place = waiting.pop(0)
                head_values(scores, whole_ref, prev_ref, out_ref, *place)
    for scores, *place in waiting:
        head_values(scores, whole_ref, prev_ref, out_ref, *place)


def relay_places():
    slots, used = {}, 0
    for stream in ("own", "prev"):
        for chunk, entry in enumerate(CHUNKS):
            for row in ROWS:
                slots[(stream, row, chunk)] = used
                used += entry[2]
    return slots, used


def number_events(tasks):
    numbers = {}
    for task in tasks:
        numbers.setdefault(task[4], len(numbers))
    return numbers


def fused(
    share_ref,
    docs_ref,
    cos_ref,
    sin_ref,
    queries_ref,
    out_ref,
    whole_ref,
    prev_ref,
    prev_docs_ref,
    relay_ref,
    q_ref,
    turned_ref,
    wide_ref,
    bias_ref,
    mixed_ref,
    send_sem,
    recv_sem,
    local_sem,
    out_sem,
):
    section = lax.axis_index("section")
    shard = lax.axis_index("ctx")
    shards = lax.axis_size("ctx")
    share_heads, rows, dim = share_ref.shape[1:]
    head_count = whole_ref.shape[1]
    y, x_hi = section // 2, section % 2
    core = shard % 2
    x_lo = shard // (shards // 2)
    inner = shard % (shards // 2)

    def along_x(way):
        flips = x_lo == (1 if way == 1 else 0)
        hi = jnp.where(flips, 1 - x_hi, x_hi)
        return hi, {"section": y * 2 + hi, "ctx": (1 - x_lo) * (shards // 2) + inner}

    x_side = {way: along_x(way) for way in (1, -1)}
    y_side = {way: {"section": ((y + way + 4) % 4) * 2 + x_hi, "ctx": shard} for way in (1, -1)}
    later = {"section": section, "ctx": (shard + 1) % shards}
    earlier = {"section": section, "ctx": (shard + shards - 1) % shards}

    query_copy = pltpu.make_async_copy(queries_ref.at[0], q_ref, local_sem.at[0])
    query_copy.start()
    own_copies = []
    for kind in (0, 1):
        target = whole_ref.at[kind, pl.ds(section * share_heads, share_heads)]
        own_copies.append(pltpu.make_async_copy(share_ref.at[kind], target, local_sem.at[3 + kind]))
        own_copies[kind].start()

    barrier = pltpu.get_barrier_semaphore()
    for device in (x_side[1][1], x_side[-1][1], y_side[1], y_side[-1], later, earlier):
        pl.semaphore_signal(barrier, inc=1, device_id=device, device_id_type=MESH)
    pl.semaphore_wait(barrier, 6)

    tasks = all_tasks()
    event_ids = number_events(tasks)
    relay_slots, _ = relay_places()

    def place_section(row, hi):
        return ((y + row + 4) % 4) * 2 + hi

    def held(stream, chunk, at):
        kind, head, heads = CHUNKS[chunk][:3]
        ref = whole_ref if stream == "own" else prev_ref
        return ref.at[kind, pl.ds(at * share_heads + head, heads)]

    def own_or_held(stream, chunk, row, other):
        kind, head, heads = CHUNKS[chunk][:3]
        if row == 0 and other == 0 and stream == "own":
            return share_ref.at[kind, pl.ds(head, heads)]
        return held(stream, chunk, place_section(row, x_hi if other == 0 else 1 - x_hi))

    def relay(stream, row, chunk):
        return relay_ref.at[pl.ds(relay_slots[(stream, row, chunk)], CHUNKS[chunk][2])]

    def ends(what):
        kind = what[0]
        if kind == "ysend":
            _, stream, block, chunk, way = what
            hi = x_hi if block == 0 else 1 - x_hi
            return own_or_held(stream, chunk, 0, block), held(stream, chunk, place_section(0, hi)), y_side[way]
        if kind == "yfwd":
            _, stream, block, chunk, way = what
            at = place_section(-way, x_hi if block == 0 else 1 - x_hi)
            return held(stream, chunk, at), held(stream, chunk, at), y_side[way]
        if kind == "xsend":
            _, stream, row, chunk, way = what
            return own_or_held(stream, chunk, row, 0), relay(stream, row, chunk), x_side[way][1]
        if kind == "xfwd":
            _, stream, row, chunk, way = what
            return relay(stream, row, chunk), held(stream, chunk, place_section(row, x_side[-way][0])), x_side[way][1]
        if kind == "shift":
            part, head, heads = CHUNKS[what[2]][:3]
            return share_ref.at[part, pl.ds(head, heads)], held("prev", what[2], section), later
        _, row, other, chunk = what
        part, head, heads = CHUNKS[chunk][:3]
        at = place_section(row, x_hi if other == 0 else 1 - x_hi)
        return own_or_held("own", chunk, row, other), prev_ref.at[part, pl.ds(at * share_heads + head, heads)], later

    def copy_of(task, number):
        source, target, device = ends(task[6])
        return pltpu.make_async_remote_copy(
            src_ref=source,
            dst_ref=target,
            send_sem=send_sem.at[number],
            recv_sem=recv_sem.at[event_ids[task[4]]],
            device_id=device,
            device_id_type=MESH,
        )

    docs_copy = pltpu.make_async_remote_copy(
        src_ref=docs_ref,
        dst_ref=prev_docs_ref,
        send_sem=local_sem.at[1],
        recv_sem=local_sem.at[2],
        device_id=later,
        device_id_type=MESH,
    )
    docs_copy.start()

    at_first, at_last = inner // 2 == 0, inner == shards // 2 - 1
    role = jnp.where(at_first, 2 + 2 * x_lo + core, jnp.where(at_last, 6 + x_lo, core))

    def clear(index, carry):
        for kind in (0, 1):
            prev_ref[kind, index] = jnp.zeros((rows, dim), prev_ref.dtype)
        return carry

    pl.when(shard == 0)(lambda: lax.fori_loop(0, prev_ref.shape[1], clear, None))

    units = {task[4]: task[3] for task in tasks}
    waited = {name: set() for name in ROLES}
    sent = {name: [] for name in ROLES}

    def wait_event(name, event):
        if event not in waited[name]:
            waited[name].add(event)
            place = relay_ref.at[pl.ds(0, units[event])]
            pltpu.make_async_copy(place, place, recv_sem.at[event_ids[event]]).wait()

    order, _ = plan(tasks)
    stages = {name: [] for name in ROLES}
    for name in ROLES:
        sends = []
        for kind, entry in role_order(order, tasks, name):
            if kind == "send":
                sends.append(entry)
            else:
                stages[name].append((sends, entry))
                sends = []
        stages[name].append((sends, None))

    def communicate(name, sends, stage):
        node = "G1" if name in ("E1", "F1") else name
        for task in sends:
            for need in task[1]:
                wait_event(name, need)
            copy_of(task, len(sent[name])).start()
            sent[name].append(task)
        if stage is not None and stage[0] == "unit":
            for need in unit_needs(node, *stage[1][1], stage[1][0]):
                wait_event(name, need)
        if stage is None:
            for task in tasks:
                if task[5] == node:
                    wait_event(name, task[4])
            for place, task in enumerate(sent[name]):
                copy_of(task, place).wait_send()

    def turn(group, carry):
        at = pl.multiple_of(group * 8, 8)
        wide_ref[...] = q_ref[:, pl.ds(at, 8), :].astype(jnp.float32).reshape(rows * 8, dim)
        for head in range(8):
            values = wide_ref[pl.ds(head, rows, stride=8), :]
            result = values * cos_ref[...] + pltpu.roll(values, dim // 2, 1) * sin_ref[...]
            turned_ref[at + head] = result.astype(jnp.bfloat16)
        return carry

    def mask():
        for copy in own_copies:
            copy.wait()
        docs_copy.wait()
        at_query = lax.broadcasted_iota(jnp.int32, (128, 128), 0)
        at_key = lax.broadcasted_iota(jnp.int32, (128, 128), 1)
        blocks = rows // 128
        prev_docs = jnp.where(shard == 0, -1, prev_docs_ref[...])
        docs = docs_ref[...]
        for block in range(blocks):
            spread = jnp.broadcast_to(docs[block : block + 1].astype(jnp.float32), (128, 128))
            query_docs = jnp.transpose(spread).astype(jnp.int32)
            for part in range(blocks + 1):
                at = block + part
                row = prev_docs[at : at + 1] if at < blocks else docs[at - blocks : at - blocks + 1]
                allowed = jnp.broadcast_to(row, (128, 128)) == query_docs
                if part == blocks:
                    allowed = jnp.logical_and(allowed, at_key <= at_query)
                bias_ref[block, :, part * 128 : part * 128 + 128] = jnp.where(allowed, 0.0, -1e30)

    for index in range(len(stages["G0"])):
        for number, name in enumerate(ROLES):
            sends, stage = stages[name][index]
            pl.when(role == number)(functools.partial(communicate, name, sends, stage))
        stage = stages["G0"][index][1]
        if stage is None:
            continue
        if stage[0] == "turn":
            if stage[1] == 0:
                query_copy.wait()
            lax.fori_loop(stage[1], stage[2], turn, 0)
        elif stage[0] == "mask":
            mask()
        else:
            base = 0
            for number, name in enumerate(ROLES):
                group, (row, other) = stages[name][index][1][1]
                at = place_section(row, x_hi if other == 0 else 1 - x_hi)
                base = jnp.where(role == number, at * share_heads + CLASSES[group][0], base)
            count = CLASSES[stage[1][0]][1]

            heads = [base + i for i in range(count)]
            softmax_heads(turned_ref, whole_ref, prev_ref, bias_ref, mixed_ref, heads)

    def narrow(index, carry):
        part = pl.ds(index * 16, 16)
        wide = mixed_ref[pl.ds(index * 16 * head_count, 16 * head_count), :]
        q_ref[part] = wide.reshape(16, head_count, dim).astype(q_ref.dtype)
        return carry

    out_copies = []
    for part in range(4):
        lax.fori_loop(part * rows // 64, (part + 1) * rows // 64, narrow, 0)
        place = pl.ds(part * rows // 4, rows // 4)
        copy = pltpu.make_async_copy(q_ref.at[place], out_ref.at[0, place], out_sem.at[part])
        copy.start()
        out_copies.append(copy)
    for copy in out_copies:
        copy.wait()


def gather_and_attend(share, documents, cosine, sine, queries, sections):
    _, heads, rows, dim = share.shape
    tasks = all_tasks()
    sends = max(sum(t[0] == name for t in tasks) for name in ROLES)
    events = len(number_events(tasks))
    head_count = heads * sections
    docs = documents.reshape(-1, 128)
    vmem = pl.BlockSpec(memory_space=pltpu.VMEM)
    anywhere = pl.BlockSpec(memory_space=pl.ANY)
    narrow = queries.dtype
    return pl.pallas_call(
        fused,
        out_shape=jax.ShapeDtypeStruct(queries.shape, narrow),
        in_specs=[anywhere, vmem, vmem, vmem, anywhere],
        out_specs=anywhere,
        scratch_shapes=[
            pltpu.VMEM((2, head_count, rows, dim), narrow),
            pltpu.VMEM((2, head_count, rows, dim), narrow),
            pltpu.VMEM(docs.shape, docs.dtype),
            pltpu.VMEM((relay_places()[1], rows, dim), narrow),
            pltpu.VMEM((rows, head_count, dim), narrow),
            pltpu.VMEM((head_count, rows, dim), narrow),
            pltpu.VMEM((rows * 8, dim), jnp.float32),
            pltpu.VMEM((rows // 128, 128, rows + 128), jnp.float32),
            pltpu.VMEM((rows * head_count, dim), jnp.float32),
            pltpu.SemaphoreType.DMA((sends,)),
            pltpu.SemaphoreType.DMA((events,)),
            pltpu.SemaphoreType.DMA((5,)),
            pltpu.SemaphoreType.DMA((4,)),
        ],
        compiler_params=pltpu.CompilerParams(collective_id=0, has_side_effects=True, vmem_limit_bytes=VMEM_LIMIT),
        name="gather_and_attend",
    )(share, docs, cosine, sine, queries)


def tables(positions, dim):
    half_dim = dim // 2
    exponent = jnp.arange(half_dim, dtype=jnp.float32) * (2.0 / dim)
    inverse = jnp.power(jnp.float32(10000.0), -exponent)
    angles = positions.astype(jnp.float32)[:, None] * inverse[None, :]
    cosine = jnp.cos(angles)
    sine = jnp.sin(angles)
    return jnp.concatenate([cosine, cosine], axis=1), jnp.concatenate([-sine, sine], axis=1)


def body(queries, keys_values, positions, documents):
    dim = queries.shape[-1]
    sections = lax.axis_size("section")
    cosine, sine = tables(positions, dim)
    by_head = jnp.transpose(keys_values, (1, 2, 0, 3))
    keys = by_head[0].astype(jnp.float32)
    swapped = jnp.concatenate([keys[..., dim // 2 :], keys[..., : dim // 2]], axis=-1)
    share = jnp.stack([(keys * cosine + swapped * sine).astype(jnp.bfloat16), by_head[1]], axis=0)
    return gather_and_attend(share, documents, cosine, sine, queries, sections)


def solution(mesh):
    placed = (P("section", "ctx", None, None), P("ctx", None, "section", None), P("ctx"), P("ctx"))
    return jax.shard_map(
        body, mesh=mesh, in_specs=placed, out_specs=P("section", "ctx", None, None), check_vma=False
    )
```
